32 devices in a mesh: section: 2 (over core), replica: 16 (over z, y, x).
Axes of the slice: x: 2, y: 2, z: 4, core: 2. Of those that a mesh axis runs over, the one named last changes fastest.
Arguments:
- tokens: bfloat16 [16, 2, 128, 1536], P('replica'), may hold values from -6 to 6
- cotangent: bfloat16 [16, 2, 128, 1536], P('replica'), may hold values from -6 to 6
- block_lengths: int32 [16, 2, 4], P('replica'), may hold values from 1 to 48, 128 in all within a row
- weights: bfloat16 [2, 16, 1536, 768], P('section', 'replica'), may hold values from -0.15625 to 0.15625
- momentum: bfloat16 [2, 16, 1536, 768], P('section', 'replica'), may hold values from -60 to 60
- step_index: int32 [1], replicated, may hold values from 0 to 63
Outputs:
- new_weights: bfloat16 [2, 16, 1536, 768], P('section', 'replica')
- new_momentum: bfloat16 [2, 16, 1536, 768], P('section', 'replica')
The draws below stay inside these ranges and needn't reach their ends.
Inputs may be any that keep to these rules, and one draw needn't show every extreme that they name: `block_lengths`: each micro-batch's 4 block lengths sum to 128.
All inputs are finite; a program needn't handle non-finite values.
Results may differ from the reference program's by a relative error of at most 0.009.
Values may be sent and summed in bfloat16 or wider, within the bound.
A program may use at most 64 MiB of HBM per device.

```python
import math
import jax
import jax.numpy as jnp
import numpy as np
from jax import lax

D = 1536
HS = 128
HD = 768
R = 128
MB = 2
BLOCKS = 4
N_SECTION = 2
N_REPLICA = 16


def steps_of(stream_key, extent, split, smallest, high):
    def one(dim, shards_of):
        steps = jax.random.uniform(jax.random.fold_in(jax.random.fold_in(stream_key, 6), dim), (shards_of,), jnp.float32, smallest / len(split), high / len(split))
        return jnp.repeat(jnp.exp(steps), extent[dim] // shards_of).reshape((-1,) + (1,) * (len(extent) - dim - 1))

    gain = one(*split[0])
    for cut in split[1:]:
        gain = gain * one(*cut)
    return gain


def split_up(number_of, total, most, lean):
    weights = [(1 << 20) // math.isqrt(grade ** lean) + 1 for grade in range(2, number_of + 1)]
    rest, counts = total - most - (number_of - 1), [1] * (number_of - 1)
    while rest > 0:
        candidates = [i for i in range(number_of - 1) if counts[i] < most]
        whole, budget = sum([weights[i] for i in candidates]), rest
        for i in candidates:
            extra = min(most - counts[i], max(1, budget * weights[i] // whole), rest)
            counts[i] = counts[i] + extra
            rest = rest - extra
    return np.array([most] + counts)


def ragged(rng, number_of, total, most, lean):
    if number_of == 2:
        one = jax.random.randint(rng, (), max(1, total - most), min(most, total - 1) + 1)
        return jnp.stack([one, total - one])
    sizes = jnp.asarray(split_up(number_of, total, most, lean), jnp.int32)
    twos = (number_of - 1) // 2
    source_of, sink = sizes[1:1 + 2 * twos:2], sizes[2:2 + 2 * twos:2]
    room = jnp.minimum(source_of - 1, most - sink)
    moved = jax.random.randint(jax.random.fold_in(rng, 1), (twos,), 0, 1 << 20) % (room + 1)
    sizes = sizes.at[1:1 + 2 * twos:2].set(source_of - moved).at[2:2 + 2 * twos:2].set(sink + moved)
    return sizes[jax.random.permutation(jax.random.fold_in(rng, 2), number_of)]


def scatter_about(stream_key, dims, spread, most, shards=(), kind=jnp.bfloat16):
    factor_of = steps_of(stream_key, dims, shards, -0.22, 0.18) if shards else 1.0
    array = jax.random.normal(stream_key, dims, jnp.float32) * spread * factor_of
    return jnp.minimum(jnp.maximum(array, -most), most).astype(kind)


def setup_inputs(seed: int = 0) -> dict:
    seeds = jax.random.split(jax.random.key(seed), 7)
    return {
        "tokens": scatter_about(seeds[0], (N_REPLICA, MB, R, D), 1.0, 6.0, ((0, 16),)),
        "cotangent": scatter_about(seeds[1], (N_REPLICA, MB, R, D), 1.0, 6.0, ((0, 16),)),
        "block_lengths": jax.vmap(lambda own: ragged(own, BLOCKS, R, 3 * R // 8, 0))(jax.random.split(seeds[2], N_REPLICA * MB)).reshape((N_REPLICA, MB, BLOCKS)).astype(jnp.int32),
        "weights": scatter_about(seeds[3], (N_SECTION, N_REPLICA, D, HD), D ** -0.5, 0.15625, ((0, 2), (1, 16))),
        "momentum": scatter_about(seeds[4], (N_SECTION, N_REPLICA, D, HD), 10.0, 60.0, ((0, 2), (1, 16))),
        "step_index": jax.random.randint(seeds[5], (1,), 0, 64).astype(jnp.int32),
    }


def visible_mask(lengths, row_count):
    bounds = jnp.cumsum(lengths.astype(jnp.int32))
    position = lax.broadcasted_iota(jnp.int32, (row_count, 1), 0)
    block_id = lax.optimization_barrier(jnp.sum((position >= bounds[None, :]).astype(jnp.int32), axis=1))
    return block_id[None, :] <= block_id[:, None]

def section_layer(inputs, weight, lengths):
    row_count = inputs.shape[0]
    head_width = weight.shape[1]
    head_count = head_width // HS
    inputs_float = inputs.astype(jnp.float32)
    normed = inputs_float * lax.rsqrt(lax.optimization_barrier(jnp.mean(inputs_float * inputs_float, axis=1, keepdims=True)) + 1e-06)
    projected = jnp.dot(normed.astype(jnp.bfloat16), weight, preferred_element_type=jnp.float32)
    heads_view = projected.reshape(row_count, head_count, HS)
    scores = jnp.einsum('qhd,khd->hqk', heads_view, heads_view) / HS
    visible = visible_mask(lengths, row_count).astype(jnp.float32)
    raised = jnp.exp(scores) * visible[None, :, :]
    attention = raised / lax.optimization_barrier(jnp.sum(raised, axis=2, keepdims=True))
    mixed_rows = jnp.einsum('hqk,khd->qhd', attention, heads_view).reshape(row_count, head_width)
    branch_out = jnp.dot(mixed_rows.astype(jnp.bfloat16), weight.T, preferred_element_type=jnp.float32)
    return (inputs_float + branch_out).astype(jnp.bfloat16)

def reference(tokens, cotangent, block_lengths, weights, momentum, step_index):
    section_total = weights.shape[0]
    micro_total = tokens.shape[1]

    def one_replica(packed):
        replica_tokens, replica_cot, replica_lengths, replica_weights = packed
        grad_list = [jnp.zeros(replica_weights.shape[1:], jnp.float32) for section_id in range(section_total)]
        for micro in range(micro_total):
            lengths = replica_lengths[micro]
            saved = []
            current = replica_tokens[micro]
            for section_id in range(section_total):
                saved.append(current)
                current = section_layer(current, replica_weights[section_id], lengths)
            upstream = replica_cot[micro]
            for section_id in reversed(range(section_total)):

                def local_fn(activation, matrix):
                    return section_layer(activation, matrix, lengths)
                unused, pullback = jax.vjp(local_fn, saved[section_id], replica_weights[section_id])
                upstream, weight_grad = pullback(upstream)
                grad_list[section_id] = grad_list[section_id] + weight_grad.astype(jnp.float32)
        return jnp.stack(grad_list, axis=0)
    grads = lax.map(one_replica, (tokens, cotangent, block_lengths, jnp.swapaxes(weights, 0, 1)))
    grads = jnp.swapaxes(grads, 0, 1)
    local = lax.optimization_barrier((0.9 * momentum.astype(jnp.float32) + grads).astype(jnp.bfloat16))
    bit_index = step_index[0] % 4
    partner = jnp.bitwise_xor(jnp.arange(N_REPLICA, dtype=jnp.int32), jnp.left_shift(jnp.int32(1), bit_index))
    local_partner = jnp.take(local, partner, axis=1)
    weight_partner = jnp.take(weights, partner, axis=1)
    moment_avg = 0.5 * (local.astype(jnp.float32) + local_partner.astype(jnp.float32))
    weight_avg = 0.5 * (weights.astype(jnp.float32) + weight_partner.astype(jnp.float32)) - 0.0005 * moment_avg
    return (weight_avg.astype(jnp.bfloat16), moment_avg.astype(jnp.bfloat16))
```

```python
from functools import partial

import jax
import jax.numpy as jnp
from jax import lax
from jax.experimental import pallas as pl
from jax.experimental.pallas import tpu as pltpu
from jax.sharding import PartitionSpec as P

HS = 128
CHUNKS = 4


F32 = jnp.float32
BF16 = jnp.bfloat16
NT = (((1,), (1,)), ((), ()))
TN = (((0,), (0,)), ((), ()))
NN = (((1,), (0,)), ((), ()))


def mm(a, b, dims=NN):
    return lax.dot_general(a, b, dims, preferred_element_type=F32)


def visible(lengths_ref, micro, rows):
    q_at = lax.broadcasted_iota(jnp.int32, (rows, rows), 0)
    k_at = lax.broadcasted_iota(jnp.int32, (rows, rows), 1)
    q_id = jnp.zeros((rows, rows), jnp.int32)
    k_id = jnp.zeros((rows, rows), jnp.int32)
    bound = jnp.int32(0)
    for block in range(lengths_ref.shape[1]):
        bound = bound + lengths_ref[micro, block]
        q_id = q_id + (q_at >= bound).astype(jnp.int32)
        k_id = k_id + (k_at >= bound).astype(jnp.int32)
    return k_id <= q_id


def normalize(x_ref):
    xf = x_ref[...].astype(F32)
    scale = lax.rsqrt(jnp.mean(xf * xf, axis=1, keepdims=True) + 1e-06)
    return xf, scale, (xf * scale).astype(BF16)


def weights_of(u_head, vis):
    raised = jnp.where(vis, jnp.exp(mm(u_head, u_head, NT) * (1.0 / HS)), 0.0)
    return raised / jnp.sum(raised, axis=1, keepdims=True)


def head_slices(micros, rows, width):
    for micro in range(micros):
        for head in range(width // HS):
            yield micro, slice(micro * rows, (micro + 1) * rows), slice(head * HS, (head + 1) * HS)


def forward_kernel(lengths_ref, x_ref, w_ref, out_ref, a_ref):
    micros = lengths_ref.shape[0]
    rows = x_ref.shape[0] // micros
    xf, _, normed = normalize(x_ref)
    u = mm(normed, w_ref[...]).astype(BF16)
    masks = [visible(lengths_ref, micro, rows) for micro in range(micros)]
    for micro, r, c in head_slices(micros, rows, w_ref.shape[1]):
        p = weights_of(u[r, c], masks[micro])
        a_ref[r, c] = mm(p.astype(BF16), u[r, c]).astype(BF16)
    out_ref[...] = (x_ref[...].astype(F32) + mm(a_ref[...], w_ref[...], NT)).astype(BF16)


def attention_back(lengths_ref, normed, d_ref, w_ref, du_ref, a_ref):
    micros = lengths_ref.shape[0]
    rows = d_ref.shape[0] // micros
    u = mm(normed, w_ref[...]).astype(BF16)
    da = mm(d_ref[...], w_ref[...]).astype(BF16)
    masks = [visible(lengths_ref, micro, rows) for micro in range(micros)]
    for micro, r, c in head_slices(micros, rows, w_ref.shape[1]):
        uh, dah = u[r, c], da[r, c]
        p = weights_of(uh, masks[micro])
        pb = p.astype(BF16)
        if a_ref is not None:
            a_ref[r, c] = mm(pb, uh).astype(BF16)
        dp = mm(dah, uh, NT)
        ds = (p * (dp - jnp.sum(dp * p, axis=1, keepdims=True)) * (1.0 / HS)).astype(BF16)
        du = mm(pb, dah, TN) + mm(ds, uh) + mm(ds, uh, TN)
        du_ref[r, c] = du.astype(BF16)


def input_grad_kernel(lengths_ref, x_ref, d_ref, w_ref, out_ref, du_ref):
    xf, scale, normed = normalize(x_ref)
    attention_back(lengths_ref, normed, d_ref, w_ref, du_ref, None)
    dn = mm(du_ref[...], w_ref[...], NT)
    xf = x_ref[...].astype(F32)
    along = jnp.mean(dn * xf, axis=1, keepdims=True)
    dx = scale * dn - xf * (scale * scale * scale * along)
    out_ref[...] = (d_ref[...].astype(F32) + dx).astype(BF16)


def local_kernel(lengths_ref, x_ref, d_ref, w_ref, m_ref, *rest):
    out_refs, (n_ref, du_ref, a_ref) = rest[:-3], rest[-3:]
    n_ref[...] = normalize(x_ref)[2]
    attention_back(lengths_ref, n_ref[...], d_ref, w_ref, du_ref, a_ref)
    size = w_ref.shape[0] // len(out_refs)
    for index, out_ref in enumerate(out_refs):
        c = slice(index * size, (index + 1) * size)
        grad = mm(n_ref[:, c], du_ref[...], TN) + mm(d_ref[:, c], a_ref[...], TN)
        out_ref[...] = (0.9 * m_ref[c, :].astype(F32) + grad).astype(BF16)


def combine_kernel(l_ref, lp_ref, w_ref, wp_ref, *rest):
    nw_ref, nm_ref = rest[-2:]
    average = 0.5 * (l_ref[...].astype(F32) + lp_ref[...].astype(F32))
    weight = 0.5 * (w_ref[...].astype(F32) + wp_ref[...].astype(F32))
    nm_ref[...] = average.astype(BF16)
    nw_ref[...] = (weight - 0.0005 * average).astype(BF16)


def vmem(count):
    return [pl.BlockSpec(memory_space=pltpu.VMEM)] * count


SMEM = [pl.BlockSpec(memory_space=pltpu.SMEM)]


def cost(flops, bytes_moved, exps):
    return pl.CostEstimate(flops=flops, bytes_accessed=bytes_moved, transcendentals=exps)


def run_forward(lengths, x, w):
    rows, width = x.shape[0], w.shape[1]
    return pl.pallas_call(
        forward_kernel,
        out_shape=jax.ShapeDtypeStruct(x.shape, BF16),
        in_specs=SMEM + vmem(2),
        out_specs=vmem(1)[0],
        scratch_shapes=[pltpu.VMEM((rows, width), BF16)],
        cost_estimate=cost(4 * rows * w.size, 2 * (w.size + 2 * x.size), rows * width),
        name="section_forward",
    )(lengths, x, w)


def run_input_grad(lengths, x, d, w):
    rows, width = x.shape[0], w.shape[1]
    return pl.pallas_call(
        input_grad_kernel,
        out_shape=jax.ShapeDtypeStruct(x.shape, BF16),
        in_specs=SMEM + vmem(3),
        out_specs=vmem(1)[0],
        scratch_shapes=[pltpu.VMEM((rows, width), BF16)],
        cost_estimate=cost(6 * rows * w.size, 2 * (w.size + 3 * x.size), rows * width),
        name="section_input_grad",
    )(lengths, x, d, w)


def run_local(lengths, x, d, w, m):
    rows, width = x.shape[0], w.shape[1]
    piece = jax.ShapeDtypeStruct((w.shape[0] // CHUNKS, width), BF16)
    return pl.pallas_call(
        local_kernel,
        out_shape=[piece] * CHUNKS,
        in_specs=SMEM + vmem(4),
        out_specs=vmem(CHUNKS),
        scratch_shapes=[
            pltpu.VMEM(x.shape, BF16),
            pltpu.VMEM((rows, width), BF16),
            pltpu.VMEM((rows, width), BF16),
        ],
        cost_estimate=cost(8 * rows * w.size, 2 * (3 * w.size + 2 * x.size), rows * width),
        name="section_local",
    )(lengths, x, d, w, m)


def run_combine(index, mine, theirs, w, wp, filled):
    size, width = mine.shape
    steps = 2
    block = size // steps
    own = pl.BlockSpec((block, width), lambda i: (i, 0))
    within = pl.BlockSpec((block, width), lambda i: (index * steps + i, 0))
    whole = jax.ShapeDtypeStruct(w.shape, BF16)
    return pl.pallas_call(
        combine_kernel,
        out_shape=[whole, whole],
        grid=(steps,),
        in_specs=[own, own, within, within] + [pl.BlockSpec(memory_space=pl.ANY)] * len(filled),
        out_specs=[within, within],
        input_output_aliases={4 + i: i for i in range(len(filled))},
        cost_estimate=cost(8 * mine.size, 12 * mine.size, 0),
        name="combine",
    )(mine, theirs, w, wp, *filled)


def partner(value, axis, stride):
    mask = 2**stride
    pairs = [(source, source ^ mask) for source in range(lax.axis_size(axis))]
    return lax.ppermute(value, axis, pairs)


def shifted(value, axis, steps):
    count = lax.axis_size(axis)
    leading, last = (max(0, -steps), min(count, count - steps))
    return lax.ppermute(value, axis, [(source, source + steps) for source in range(leading, last)])


def step(bit, tokens, cotangent, lengths, weight, momentum):
    sections = lax.axis_size("section")
    here = lax.axis_index("section")
    theirs = partner(weight, "replica", bit)
    x, d = tokens, cotangent
    for tick in range(sections - 1):
        arriving = shifted(run_forward(lengths, x, weight), "section", 1)
        x = jnp.where(here == tick + 1, arriving, x)
    for tick in range(sections - 1):
        arriving = shifted(run_input_grad(lengths, x, d, weight), "section", -1)
        d = jnp.where(here == sections - 2 - tick, arriving, d)
    pieces = run_local(lengths, x, d, weight, momentum)
    others = [partner(piece, "replica", bit) for piece in pieces]
    filled = ()
    for index in range(CHUNKS):
        filled = run_combine(index, pieces[index], others[index], weight, theirs, filled)
    return tuple(filled)


def per_device(tokens, cotangent, block_lengths, weights, momentum, step_index):
    rows = tokens.shape[1] * tokens.shape[2]
    wide = tokens.shape[3]
    new_weight, new_momentum = lax.switch(
        step_index[0] % 4,
        [partial(step, bit) for bit in range(4)],
        tokens.reshape(rows, wide),
        cotangent.reshape(rows, wide),
        block_lengths[0],
        weights[0, 0],
        momentum[0, 0],
    )
    return new_weight[None, None], new_momentum[None, None]


def solution(mesh):
    in_specs = (
        P("replica", None, None, None),
        P("replica", None, None, None),
        P("replica", None, None),
        P("section", "replica", None, None),
        P("section", "replica", None, None),
        P(),
    )
    out_specs = (P("section", "replica", None, None), P("section", "replica", None, None))
    return jax.shard_map(
        per_device, mesh=mesh, in_specs=in_specs, out_specs=out_specs, check_vma=False
    )
```

```python
from functools import partial

import jax
import jax.numpy as jnp
from jax import lax
from jax.experimental import pallas as pl
from jax.experimental.pallas import tpu as pltpu
from jax.sharding import PartitionSpec as P

HS = 128
SHARES = (5, 4, 2, 1)


F32 = jnp.float32
BF16 = jnp.bfloat16
NT = (((1,), (1,)), ((), ()))
TN = (((0,), (0,)), ((), ()))
NN = (((1,), (0,)), ((), ()))


def mm(a, b, dims=NN):
    return lax.dot_general(a, b, dims, preferred_element_type=F32)


def visible(lengths_ref, micro, rows):
    q_at = lax.broadcasted_iota(jnp.int32, (rows, rows), 0)
    k_at = lax.broadcasted_iota(jnp.int32, (rows, rows), 1)
    q_id = jnp.zeros((rows, rows), jnp.int32)
    k_id = jnp.zeros((rows, rows), jnp.int32)
    bound = jnp.int32(0)
    for block in range(lengths_ref.shape[1]):
        bound = bound + lengths_ref[micro, block]
        q_id = q_id + (q_at >= bound).astype(jnp.int32)
        k_id = k_id + (k_at >= bound).astype(jnp.int32)
    return k_id <= q_id


def normalize(x_ref, n_ref):
    def rows(r):
        xf = x_ref[r, :].astype(F32)
        scale = lax.rsqrt(jnp.mean(xf * xf, axis=1, keepdims=True) + 1e-06)
        n_ref[r, :] = (xf * scale).astype(BF16)

    each_block(x_ref.shape[0], 32, rows)


def weights_of(u_head, vis):
    raised = jnp.where(vis, jnp.exp(mm(u_head, u_head, NT) * (1.0 / HS)), 0.0)
    return raised / jnp.sum(raised, axis=1, keepdims=True)


def block_of(extent):
    return 256 if extent % 256 == 0 else HS


def each_block(extent, size, body):
    def once(index, carry):
        body(pl.ds(pl.multiple_of(index * size, size), size))
        return carry

    lax.fori_loop(0, extent // size, once, 0)


def project(out_ref, left_ref, w_ref):
    def body(c):
        out_ref[:, c] = mm(left_ref[...], w_ref[:, c]).astype(BF16)

    each_block(w_ref.shape[1], block_of(w_ref.shape[1]), body)


def each_head(lengths_ref, rows_all, width, body):
    micros = lengths_ref.shape[0]
    rows = rows_all // micros
    masks = [visible(lengths_ref, micro, rows) for micro in range(micros)]

    def heads(c):
        for micro in range(micros):
            body(slice(micro * rows, (micro + 1) * rows), c, masks[micro])

    each_block(width, HS, heads)


def forward_kernel(lengths_ref, x_ref, w_ref, out_ref, n_ref, u_ref, a_ref):
    normalize(x_ref, n_ref)
    project(u_ref, n_ref, w_ref)

    def head(r, c, mask):
        uh = u_ref[r, c]
        a_ref[r, c] = mm(weights_of(uh, mask).astype(BF16), uh).astype(BF16)

    each_head(lengths_ref, x_ref.shape[0], w_ref.shape[1], head)

    def body(c):
        out = x_ref[:, c].astype(F32) + mm(a_ref[...], w_ref[c, :], NT)
        out_ref[:, c] = out.astype(BF16)

    each_block(w_ref.shape[0], block_of(w_ref.shape[0]), body)


def attention_back(lengths_ref, n_ref, d_ref, w_ref, u_ref, da_ref, du_ref, a_ref):
    project(u_ref, n_ref, w_ref)
    project(da_ref, d_ref, w_ref)

    def head(r, c, mask):
        uh, dah = u_ref[r, c], da_ref[r, c]
        p = weights_of(uh, mask)
        pb = p.astype(BF16)
        if a_ref is not None:
            a_ref[r, c] = mm(pb, uh).astype(BF16)
        dp = mm(dah, uh, NT)
        ds = (p * (dp - jnp.sum(dp * p, axis=1, keepdims=True)) * (1.0 / HS)).astype(BF16)
        du = mm(pb, dah, TN) + mm(ds, uh) + mm(ds, uh, TN)
        du_ref[r, c] = du.astype(BF16)

    each_head(lengths_ref, d_ref.shape[0], w_ref.shape[1], head)


def input_grad_kernel(lengths_ref, x_ref, d_ref, w_ref, out_ref, n_ref, u_ref, da_ref, du_ref, dn_ref):
    normalize(x_ref, n_ref)
    attention_back(lengths_ref, n_ref, d_ref, w_ref, u_ref, da_ref, du_ref, None)

    def body(c):
        dn_ref[:, c] = mm(du_ref[...], w_ref[c, :], NT)

    each_block(w_ref.shape[0], block_of(w_ref.shape[0]), body)

    def rows(r):
        xf = x_ref[r, :].astype(F32)
        dn = dn_ref[r, :]
        scale = lax.rsqrt(jnp.mean(xf * xf, axis=1, keepdims=True) + 1e-06)
        along = jnp.mean(dn * xf, axis=1, keepdims=True)
        dx = scale * dn - xf * (scale * scale * scale * along)
        out_ref[r, :] = (d_ref[r, :].astype(F32) + dx).astype(BF16)

    each_block(x_ref.shape[0], 32, rows)


def local_kernel(lengths_ref, x_ref, d_ref, w_ref, m_ref, *rest):
    out_refs, (n_ref, u_ref, da_ref, du_ref, a_ref) = rest[:-5], rest[-5:]
    normalize(x_ref, n_ref)
    attention_back(lengths_ref, n_ref, d_ref, w_ref, u_ref, da_ref, du_ref, a_ref)
    start = 0
    for out_ref in out_refs:

        def once(index, carry, start=start, out_ref=out_ref):
            c = pl.ds(pl.multiple_of(start + index * HS, HS), HS)
            r = pl.ds(pl.multiple_of(index * HS, HS), HS)
            grad = mm(n_ref[:, c], du_ref[...], TN) + mm(d_ref[:, c], a_ref[...], TN)
            out_ref[r, :] = (0.9 * m_ref[c, :].astype(F32) + grad).astype(BF16)
            return carry

        lax.fori_loop(0, out_ref.shape[0] // HS, once, 0)
        start += out_ref.shape[0]


def combine_kernel(l_ref, lp_ref, w_ref, wp_ref, *rest):
    nw_ref, nm_ref = rest[-2:]
    average = 0.5 * (l_ref[...].astype(F32) + lp_ref[...].astype(F32))
    weight = 0.5 * (w_ref[...].astype(F32) + wp_ref[...].astype(F32))
    nm_ref[...] = average.astype(BF16)
    nw_ref[...] = (weight - 0.0005 * average).astype(BF16)


def vmem(count):
    return [pl.BlockSpec(memory_space=pltpu.VMEM)] * count


SMEM = [pl.BlockSpec(memory_space=pltpu.SMEM)]


def cost(flops, bytes_moved, exps):
    return pl.CostEstimate(flops=flops, bytes_accessed=bytes_moved, transcendentals=exps)


def scratch(x, width, count):
    return [pltpu.VMEM(x.shape, BF16)] + [pltpu.VMEM((x.shape[0], width), BF16)] * count


def sizes_of(total):
    unit = total // sum(SHARES)
    return [share * unit for share in SHARES]


def run_forward(lengths, x, w):
    rows, width = x.shape[0], w.shape[1]
    return pl.pallas_call(
        forward_kernel,
        out_shape=jax.ShapeDtypeStruct(x.shape, BF16),
        in_specs=SMEM + vmem(2),
        out_specs=vmem(1)[0],
        scratch_shapes=scratch(x, width, 2),
        cost_estimate=cost(4 * rows * w.size, 2 * (w.size + 2 * x.size), rows * width),
        name="section_forward",
    )(lengths, x, w)


def run_input_grad(lengths, x, d, w):
    rows, width = x.shape[0], w.shape[1]
    return pl.pallas_call(
        input_grad_kernel,
        out_shape=jax.ShapeDtypeStruct(x.shape, BF16),
        in_specs=SMEM + vmem(3),
        out_specs=vmem(1)[0],
        scratch_shapes=scratch(x, width, 3) + [pltpu.VMEM(x.shape, F32)],
        cost_estimate=cost(6 * rows * w.size, 2 * (w.size + 3 * x.size), rows * width),
        name="section_input_grad",
    )(lengths, x, d, w)


def run_local(lengths, x, d, w, m):
    rows, width = x.shape[0], w.shape[1]
    sizes = sizes_of(w.shape[0])
    return pl.pallas_call(
        local_kernel,
        out_shape=[jax.ShapeDtypeStruct((size, width), BF16) for size in sizes],
        in_specs=SMEM + vmem(4),
        out_specs=vmem(len(sizes)),
        scratch_shapes=scratch(x, width, 4),
        cost_estimate=cost(8 * rows * w.size, 2 * (3 * w.size + 2 * x.size), rows * width),
        name="section_local",
    )(lengths, x, d, w, m)


def run_combine(start, mine, theirs, w, wp, filled):
    size, width = mine.shape
    block = HS
    first = start // block
    own = pl.BlockSpec((block, width), lambda i: (i, 0))
    within = pl.BlockSpec((block, width), lambda i: (first + i, 0))
    whole = jax.ShapeDtypeStruct(w.shape, BF16)
    return pl.pallas_call(
        combine_kernel,
        out_shape=[whole, whole],
        grid=(size // block,),
        in_specs=[own, own, within, within] + [pl.BlockSpec(memory_space=pl.ANY)] * len(filled),
        out_specs=[within, within],
        input_output_aliases={4 + i: i for i in range(len(filled))},
        cost_estimate=cost(8 * mine.size, 12 * mine.size, 0),
        name="combine",
    )(mine, theirs, w, wp, *filled)


def partner(value, axis, stride):
    mask = 2**stride
    pairs = [(source, source ^ mask) for source in range(lax.axis_size(axis))]
    return lax.ppermute(value, axis, pairs)


def shifted(value, axis, steps):
    count = lax.axis_size(axis)
    leading, last = (max(0, -steps), min(count, count - steps))
    return lax.ppermute(value, axis, [(source, source + steps) for source in range(leading, last)])


def step(bit, tokens, cotangent, lengths, weight, momentum):
    sections = lax.axis_size("section")
    here = lax.axis_index("section")
    theirs = partner(weight, "replica", bit)
    x, d = tokens, cotangent
    for tick in range(sections - 1):
        leaving = run_forward(lengths, x, weight)
        arriving = shifted(leaving, "section", 1)
        x = jnp.where(here == tick + 1, arriving, x)
    for tick in range(sections - 1):
        arriving = shifted(run_input_grad(lengths, x, d, weight), "section", -1)
        d = jnp.where(here == sections - 2 - tick, arriving, d)
    pieces = run_local(lengths, x, d, weight, momentum)
    others = [partner(piece, "replica", bit) for piece in pieces]
    filled, start = (), 0
    for mine, other in zip(pieces[:-1], others[:-1]):
        filled = run_combine(start, mine, other, weight, theirs, filled)
        start += mine.shape[0]
    return (*filled, pieces[-1], others[-1], theirs)


def per_device(tokens, cotangent, block_lengths, weights, momentum, step_index):
    rows = tokens.shape[1] * tokens.shape[2]
    wide = tokens.shape[3]
    weight = weights[0, 0]
    *filled, mine, other, theirs = lax.switch(
        step_index[0] % 4,
        [partial(step, bit) for bit in range(4)],
        tokens.reshape(rows, wide),
        cotangent.reshape(rows, wide),
        block_lengths[0],
        weight,
        momentum[0, 0],
    )
    new_weight, new_momentum = run_combine(
        weight.shape[0] - mine.shape[0], mine, other, weight, theirs, filled
    )
    return new_weight[None, None], new_momentum[None, None]


def solution(mesh):
    in_specs = (
        P("replica", None, None, None),
        P("replica", None, None, None),
        P("replica", None, None),
        P("section", "replica", None, None),
        P("section", "replica", None, None),
        P(),
    )
    out_specs = (P("section", "replica", None, None), P("section", "replica", None, None))
    return jax.shard_map(
        per_device, mesh=mesh, in_specs=in_specs, out_specs=out_specs, check_vma=False
    )
```

```python
from functools import partial

import jax
import jax.numpy as jnp
from jax import lax
from jax.experimental import pallas as pl
from jax.experimental.pallas import tpu as pltpu
from jax.sharding import PartitionSpec as P

HS = 128
SHARES = (5, 4, 2, 1)
ROWS_UNROLL = 4
HEADS_UNROLL = 2


F32 = jnp.float32
BF16 = jnp.bfloat16
NT = (((1,), (1,)), ((), ()))
TN = (((0,), (0,)), ((), ()))
NN = (((1,), (0,)), ((), ()))


def mm(a, b, dims=NN):
    return lax.dot_general(a, b, dims, preferred_element_type=F32)


def visible(lengths_ref, micro, rows):
    q_at = lax.broadcasted_iota(jnp.int32, (rows, rows), 0)
    k_at = lax.broadcasted_iota(jnp.int32, (rows, rows), 1)
    q_id = jnp.zeros((rows, rows), jnp.int32)
    k_id = jnp.zeros((rows, rows), jnp.int32)
    bound = jnp.int32(0)
    for block in range(lengths_ref.shape[1]):
        bound = bound + lengths_ref[micro, block]
        q_id = q_id + (q_at >= bound).astype(jnp.int32)
        k_id = k_id + (k_at >= bound).astype(jnp.int32)
    return k_id <= q_id


def normalize(x_ref, n_ref):
    def rows(r):
        xf = x_ref[r, :].astype(F32)
        scale = lax.rsqrt(jnp.mean(xf * xf, axis=1, keepdims=True) + 1e-06)
        n_ref[r, :] = (xf * scale).astype(BF16)

    each_block(x_ref.shape[0], 32, rows, ROWS_UNROLL)


def weights_of(u_head, vis):
    raised = jnp.where(vis, jnp.exp(mm(u_head, u_head, NT) * (1.0 / HS)), 0.0)
    return raised / jnp.sum(raised, axis=1, keepdims=True)


def block_of(extent):
    return 256 if extent % 256 == 0 else HS


def each_block(extent, size, body, unroll=1):
    def once(index, carry):
        body(pl.ds(pl.multiple_of(index * size, size), size))
        return carry

    lax.fori_loop(0, extent // size, once, 0, unroll=unroll)


def project(out_ref, left_ref, w_ref):
    def body(c):
        out_ref[:, c] = mm(left_ref[...], w_ref[:, c]).astype(BF16)

    each_block(w_ref.shape[1], block_of(w_ref.shape[1]), body)


def each_head(lengths_ref, rows_all, width, body):
    micros = lengths_ref.shape[0]
    rows = rows_all // micros
    masks = [visible(lengths_ref, micro, rows) for micro in range(micros)]

    def heads(c):
        for micro in range(micros):
            body(slice(micro * rows, (micro + 1) * rows), c, masks[micro])

    each_block(width, HS, heads, HEADS_UNROLL)


def forward_kernel(lengths_ref, x_ref, w_ref, out_ref, n_ref, u_ref, a_ref):
    normalize(x_ref, n_ref)
    project(u_ref, n_ref, w_ref)

    def head(r, c, mask):
        uh = u_ref[r, c]
        a_ref[r, c] = mm(weights_of(uh, mask).astype(BF16), uh).astype(BF16)

    each_head(lengths_ref, x_ref.shape[0], w_ref.shape[1], head)

    def body(c):
        out = x_ref[:, c].astype(F32) + mm(a_ref[...], w_ref[c, :], NT)
        out_ref[:, c] = out.astype(BF16)

    each_block(w_ref.shape[0], block_of(w_ref.shape[0]), body)


def attention_back(lengths_ref, n_ref, d_ref, w_ref, u_ref, da_ref, du_ref, a_ref):
    project(u_ref, n_ref, w_ref)
    project(da_ref, d_ref, w_ref)

    def head(r, c, mask):
        uh, dah = u_ref[r, c], da_ref[r, c]
        p = weights_of(uh, mask)
        pb = p.astype(BF16)
        if a_ref is not None:
            a_ref[r, c] = mm(pb, uh).astype(BF16)
        dp = mm(dah, uh, NT)
        ds = (p * (dp - jnp.sum(dp * p, axis=1, keepdims=True)) * (1.0 / HS)).astype(BF16)
        du = mm(pb, dah, TN) + mm(ds, uh) + mm(ds, uh, TN)
        du_ref[r, c] = du.astype(BF16)

    each_head(lengths_ref, d_ref.shape[0], w_ref.shape[1], head)


def input_grad_kernel(lengths_ref, x_ref, d_ref, w_ref, out_ref, n_ref, u_ref, da_ref, du_ref, dn_ref):
    normalize(x_ref, n_ref)
    attention_back(lengths_ref, n_ref, d_ref, w_ref, u_ref, da_ref, du_ref, None)

    def body(c):
        dn_ref[:, c] = mm(du_ref[...], w_ref[c, :], NT)

    each_block(w_ref.shape[0], block_of(w_ref.shape[0]), body)

    def rows(r):
        xf = x_ref[r, :].astype(F32)
        dn = dn_ref[r, :]
        scale = lax.rsqrt(jnp.mean(xf * xf, axis=1, keepdims=True) + 1e-06)
        along = jnp.mean(dn * xf, axis=1, keepdims=True)
        dx = scale * dn - xf * (scale * scale * scale * along)
        out_ref[r, :] = (d_ref[r, :].astype(F32) + dx).astype(BF16)

    each_block(x_ref.shape[0], 32, rows, ROWS_UNROLL)


def local_kernel(lengths_ref, x_ref, d_ref, w_ref, m_ref, *rest):
    out_refs, (n_ref, u_ref, da_ref, du_ref, a_ref) = rest[:-5], rest[-5:]
    normalize(x_ref, n_ref)
    attention_back(lengths_ref, n_ref, d_ref, w_ref, u_ref, da_ref, du_ref, a_ref)
    start = 0
    for out_ref in out_refs:

        def once(index, carry, start=start, out_ref=out_ref):
            c = pl.ds(pl.multiple_of(start + index * HS, HS), HS)
            r = pl.ds(pl.multiple_of(index * HS, HS), HS)
            grad = mm(n_ref[:, c], du_ref[...], TN) + mm(d_ref[:, c], a_ref[...], TN)
            out_ref[r, :] = (0.9 * m_ref[c, :].astype(F32) + grad).astype(BF16)
            return carry

        lax.fori_loop(0, out_ref.shape[0] // HS, once, 0)
        start += out_ref.shape[0]


def combine_kernel(l_ref, lp_ref, w_ref, wp_ref, *rest):
    nw_ref, nm_ref = rest[-2:]
    average = 0.5 * (l_ref[...].astype(F32) + lp_ref[...].astype(F32))
    weight = 0.5 * (w_ref[...].astype(F32) + wp_ref[...].astype(F32))
    nm_ref[...] = average.astype(BF16)
    nw_ref[...] = (weight - 0.0005 * average).astype(BF16)


def vmem(count):
    return [pl.BlockSpec(memory_space=pltpu.VMEM)] * count


SMEM = [pl.BlockSpec(memory_space=pltpu.SMEM)]


def cost(flops, bytes_moved, exps):
    return pl.CostEstimate(flops=flops, bytes_accessed=bytes_moved, transcendentals=exps)


def scratch(x, width, count):
    return [pltpu.VMEM(x.shape, BF16)] + [pltpu.VMEM((x.shape[0], width), BF16)] * count


def sizes_of(total):
    unit = total // sum(SHARES)
    return [share * unit for share in SHARES]


def run_forward(lengths, x, w):
    rows, width = x.shape[0], w.shape[1]
    return pl.pallas_call(
        forward_kernel,
        out_shape=jax.ShapeDtypeStruct(x.shape, BF16),
        in_specs=SMEM + vmem(2),
        out_specs=vmem(1)[0],
        scratch_shapes=scratch(x, width, 2),
        cost_estimate=cost(4 * rows * w.size, 2 * (w.size + 2 * x.size), rows * width),
        name="section_forward",
    )(lengths, x, w)


def run_input_grad(lengths, x, d, w):
    rows, width = x.shape[0], w.shape[1]
    return pl.pallas_call(
        input_grad_kernel,
        out_shape=jax.ShapeDtypeStruct(x.shape, BF16),
        in_specs=SMEM + vmem(3),
        out_specs=vmem(1)[0],
        scratch_shapes=scratch(x, width, 3) + [pltpu.VMEM(x.shape, F32)],
        cost_estimate=cost(6 * rows * w.size, 2 * (w.size + 3 * x.size), rows * width),
        name="section_input_grad",
    )(lengths, x, d, w)


def run_local(lengths, x, d, w, m):
    rows, width = x.shape[0], w.shape[1]
    sizes = sizes_of(w.shape[0])
    return pl.pallas_call(
        local_kernel,
        out_shape=[jax.ShapeDtypeStruct((size, width), BF16) for size in sizes],
        in_specs=SMEM + vmem(4),
        out_specs=vmem(len(sizes)),
        scratch_shapes=scratch(x, width, 4),
        cost_estimate=cost(8 * rows * w.size, 2 * (3 * w.size + 2 * x.size), rows * width),
        name="section_local",
    )(lengths, x, d, w, m)


def run_combine(start, mine, theirs, w, wp, filled):
    size, width = mine.shape
    block = HS
    first = start // block
    own = pl.BlockSpec((block, width), lambda i: (i, 0))
    within = pl.BlockSpec((block, width), lambda i: (first + i, 0))
    whole = jax.ShapeDtypeStruct(w.shape, BF16)
    return pl.pallas_call(
        combine_kernel,
        out_shape=[whole, whole],
        grid=(size // block,),
        in_specs=[own, own, within, within] + [pl.BlockSpec(memory_space=pl.ANY)] * len(filled),
        out_specs=[within, within],
        input_output_aliases={4 + i: i for i in range(len(filled))},
        cost_estimate=cost(8 * mine.size, 12 * mine.size, 0),
        name="combine",
    )(mine, theirs, w, wp, *filled)


def partner(value, axis, stride):
    mask = 2**stride
    pairs = [(source, source ^ mask) for source in range(lax.axis_size(axis))]
    return lax.ppermute(value, axis, pairs)


def shifted(value, axis, steps):
    count = lax.axis_size(axis)
    leading, last = (max(0, -steps), min(count, count - steps))
    return lax.ppermute(value, axis, [(source, source + steps) for source in range(leading, last)])


def step(bit, tokens, cotangent, lengths, weight, momentum):
    sections = lax.axis_size("section")
    here = lax.axis_index("section")
    theirs = partner(weight, "replica", bit)
    x, d = tokens, cotangent
    for tick in range(sections - 1):
        leaving = run_forward(lengths, x, weight)
        arriving = shifted(leaving, "section", 1)
        x = jnp.where(here == tick + 1, arriving, x)
    for tick in range(sections - 1):
        arriving = shifted(run_input_grad(lengths, x, d, weight), "section", -1)
        d = jnp.where(here == sections - 2 - tick, arriving, d)
    pieces = run_local(lengths, x, d, weight, momentum)
    others = [partner(piece, "replica", bit) for piece in pieces]
    filled, start = (), 0
    for mine, other in zip(pieces[:-1], others[:-1]):
        filled = run_combine(start, mine, other, weight, theirs, filled)
        start += mine.shape[0]
    return (*filled, pieces[-1], others[-1], theirs)


def per_device(tokens, cotangent, block_lengths, weights, momentum, step_index):
    rows = tokens.shape[1] * tokens.shape[2]
    wide = tokens.shape[3]
    weight = weights[0, 0]
    *filled, mine, other, theirs = lax.switch(
        step_index[0] % 4,
        [partial(step, bit) for bit in range(4)],
        tokens.reshape(rows, wide),
        cotangent.reshape(rows, wide),
        block_lengths[0],
        weight,
        momentum[0, 0],
    )
    new_weight, new_momentum = run_combine(
        weight.shape[0] - mine.shape[0], mine, other, weight, theirs, filled
    )
    return new_weight[None, None], new_momentum[None, None]


def solution(mesh):
    in_specs = (
        P("replica", None, None, None),
        P("replica", None, None, None),
        P("replica", None, None),
        P("section", "replica", None, None),
        P("section", "replica", None, None),
        P(),
    )
    out_specs = (P("section", "replica", None, None), P("section", "replica", None, None))
    return jax.shard_map(
        per_device, mesh=mesh, in_specs=in_specs, out_specs=out_specs, check_vma=False
    )
```
